512 devices in a mesh: dp: 8 (over y, core), seq: 64 (over x, z).
Axes of the slice: x: 4, y: 4, z: 16, core: 2. Of those that a mesh axis runs over, the one named last changes fastest.
Arguments:
- queries: bfloat16 [8, 4096, 8192], P('dp', 'seq'), may hold values from -8 to 8
- keys: bfloat16 [8, 4096, 1024], P('dp', 'seq'), may hold values from -8 to 8
- values: bfloat16 [8, 4096, 1024], P('dp', 'seq'), may hold values from -6 to 6
- doc_lengths: int32 [8, 129], replicated, may hold values from 0 to 2048, as said below
Outputs:
- attended: bfloat16 [8, 4096, 8192], P('dp', 'seq')
The draws below stay inside these ranges and needn't reach their ends.
Inputs may be any that keep to these rules, and one draw needn't show every extreme that they name: `doc_lengths`: each row sums to 4096; zeros stand only after the last document; the first document of every row has 32 tokens and the second exactly 2048.
All inputs are finite; a program needn't handle non-finite values.
Results may differ from the reference program's by a relative error of at most 0.0045.
Values may be sent and summed in bfloat16 or wider, within the bound.
A program may use at most 64 MiB of HBM per device.

```python
import math
import jax
import jax.numpy as jnp
from jax import lax

QH = 64
KVH = 8
HD = 128
TOK_DEV = 64
GROUP = 8
SEQS = 8
LEN = 4096
MAXDOC = 2048
DOCS = 129


def draw_queries(key, part):
    drawn = jnp.clip(jax.random.normal(jax.random.fold_in(key, 1), (SEQS, LEN, QH * HD), jnp.float32), -4.5, 4.5)
    return drawn.astype(jnp.bfloat16)


def draw_keys(key, part):
    drawn = jnp.clip(jax.random.normal(jax.random.fold_in(key, 2), (SEQS, LEN, KVH * HD), jnp.float32), -4.5, 4.5)
    return drawn.astype(jnp.bfloat16)


def draw_doc_lengths(key, part):
    scale_key, raw_key = jax.random.split(jax.random.fold_in(key, 5))
    lowest = max(1, MAXDOC // 64)
    level = jax.random.randint(scale_key, (SEQS, 1), 0, 6)
    typical = jnp.right_shift(jnp.full((SEQS, 1), MAXDOC, jnp.int32), level.astype(jnp.int32))
    low_end = jnp.maximum(typical // 2, lowest)
    high_end = jnp.minimum(2 * typical, MAXDOC)
    spread = jax.random.randint(raw_key, (SEQS, DOCS), 0, 1 << 20)
    raw = low_end + spread % (high_end - low_end + 1)
    raw = raw.at[:, 0].set(max(1, TOK_DEV // 2))
    raw = raw.at[:, 1].set(MAXDOC)
    doc_ends = jnp.cumsum(raw, axis=1)
    doc_begins = doc_ends - raw
    return jnp.clip(LEN - doc_begins, 0, raw).astype(jnp.int32)


def shard_levels(stream_key, dims, cuts, smallest, high):
    def one(dim, parts):
        steps = jax.random.uniform(jax.random.fold_in(jax.random.fold_in(stream_key, 6), dim), (parts,), jnp.float32, smallest / len(cuts), high / len(cuts))
        return jnp.repeat(jnp.exp(steps), dims[dim] // parts).reshape((-1,) + (1,) * (len(dims) - dim - 1))

    gain = one(*cuts[0])
    for cut in cuts[1:]:
        gain = gain * one(*cut)
    return gain


def gaussian(stream_key, shape, width, bound, cuts=(), kind=jnp.bfloat16):
    factor_of = shard_levels(stream_key, shape, cuts, -0.22, 0.18) if cuts else 1.0
    entries = jax.random.normal(stream_key, shape, jnp.float32) * width * factor_of
    return jnp.minimum(jnp.maximum(entries, -bound), bound).astype(kind)


def setup_inputs(seed: int = 0) -> dict:
    streams_of = jax.random.split(jax.random.key(seed), 5)
    queries = draw_queries(jax.random.fold_in(streams_of[4], 71), 0)
    keys = draw_keys(jax.random.fold_in(streams_of[4], 71), 0)
    values = gaussian(streams_of[2], (SEQS, LEN, KVH * HD), 1.0, 6.0, ((0, 8), (1, 64)))
    doc_lengths = draw_doc_lengths(jax.random.fold_in(streams_of[4], 71), 0)
    return dict(queries=queries, keys=keys, values=values, doc_lengths=doc_lengths)


def doc_starts(lengths_row, positions):
    doc_ends = jnp.cumsum(lengths_row).astype(jnp.int32)
    return lax.optimization_barrier(jnp.max(jnp.where(doc_ends[None, :] <= positions[:, None], doc_ends, 0), axis=1)).astype(jnp.int32)

def one_sequence(operands):
    seq_queries, seq_keys, seq_values, lengths_row = operands
    block_rows = min(512, LEN)
    window = MAXDOC + block_rows
    score_scale = 1.0 / math.sqrt(HD)
    grouped = seq_queries.reshape(LEN, KVH, GROUP, HD)
    padded_keys = jnp.concatenate([jnp.zeros((MAXDOC, KVH * HD), seq_keys.dtype), seq_keys], axis=0).reshape(MAXDOC + LEN, KVH, HD)
    padded_values = jnp.concatenate([jnp.zeros((MAXDOC, KVH * HD), seq_values.dtype), seq_values], axis=0).reshape(MAXDOC + LEN, KVH, HD)

    def one_block(block_index):
        first_row = (block_index * block_rows).astype(jnp.int32)
        query_block = lax.dynamic_slice_in_dim(grouped, first_row, block_rows, 0).astype(jnp.float32)
        key_window = lax.dynamic_slice_in_dim(padded_keys, first_row, window, 0).astype(jnp.float32)
        value_window = lax.dynamic_slice_in_dim(padded_values, first_row, window, 0).astype(jnp.float32)
        positions = first_row + jnp.arange(block_rows, dtype=jnp.int32)
        key_positions = first_row - MAXDOC + jnp.arange(window, dtype=jnp.int32)
        starts = doc_starts(lengths_row, positions)
        allowed = (key_positions[None, :] >= starts[:, None]) & (key_positions[None, :] <= positions[:, None])
        scores = jnp.einsum('qkgd,tkd->kgqt', query_block, key_window, precision=lax.Precision.HIGHEST) * score_scale
        masked = jnp.where(allowed[None, None], scores, -jnp.inf)
        peak = lax.optimization_barrier(jnp.max(masked, axis=-1, keepdims=True))
        weights = jnp.where(allowed[None, None], jnp.exp(scores - peak), 0.0).astype(jnp.bfloat16)
        weights_wide = weights.astype(jnp.float32)
        total = lax.optimization_barrier(jnp.sum(weights_wide, axis=-1))
        summed = jnp.einsum('kgqt,tkd->qkgd', weights_wide, value_window, precision=lax.Precision.HIGHEST)
        result = summed / jnp.transpose(total, (2, 0, 1))[..., None]
        return result.astype(jnp.bfloat16).reshape(block_rows, QH * HD)
    blocks = lax.map(one_block, jnp.arange(LEN // block_rows, dtype=jnp.int32))
    return blocks.reshape(LEN, QH * HD)

def reference(queries, keys, values, doc_lengths):
    return lax.map(one_sequence, (queries, keys, values, doc_lengths))
```

```python
import functools
import math

import jax
import jax.numpy as jnp
from jax import lax
from jax.experimental import pallas as pl
from jax.experimental.pallas import tpu as pltpu
from jax.sharding import PartitionSpec as P

QH = 64
KVH = 8
HD = 128
GROUP = 8
XN = 4
NEG = -1e30
MESH = pl.DeviceIdType.MESH


def kernel(
    zn, tok, q_ref, k_ref, v_ref, len_ref, o_ref,
    qbuf, kvbuf, obuf, acc, mx, sm, starts,
    kv_ssem, kv_rsem, kv_lsem, q_ssem, q_rsem, q_lsem,
    rt_ssem, rt_rsem, lf_ssem, lf_rsem, o_ssem, o_rsem, o_lsem,
):
    me = lax.axis_index("seq")
    x, z = me // zn, me % zn
    dp = lax.axis_index("dp")
    up = x * zn + (z + 1) % zn
    down = x * zn + (z + zn - 1) % zn
    scale2 = math.log2(math.e) / math.sqrt(HD)
    half_ring = zn // 2
    kvw = GROUP * HD

    def peer(d):
        return (x + d) % XN

    barrier = pltpu.get_barrier_semaphore()
    for other in [up, down] + [peer(d) * zn + z for d in range(1, XN)]:
        pl.semaphore_signal(barrier, inc=1, device_id={"seq": other}, device_id_type=MESH)
    pl.semaphore_wait(barrier, XN + 1)

    def kv_copy(d, h, which):
        src = (k_ref, v_ref)[which]
        to = peer(d)
        lane = pl.multiple_of((to * 2 + h) * HD, HD)
        return pltpu.make_async_remote_copy(
            src_ref=src.at[0, :, pl.ds(lane, HD)],
            dst_ref=kvbuf.at[h, x // 2, z, which, x % 2],
            send_sem=kv_ssem.at[d - 1, h, which],
            recv_sem=kv_rsem.at[d - 1, h, which],
            device_id={"seq": to * zn + z},
            device_id_type=MESH,
        )

    def kv_own(h, which):
        src = (k_ref, v_ref)[which]
        lane = pl.multiple_of((x * 2 + h) * HD, HD)
        return pltpu.make_async_copy(
            src.at[0, :, pl.ds(lane, HD)],
            kvbuf.at[h, x // 2, z, which, x % 2],
            kv_lsem.at[h, which],
        )

    def q_copy(d, h):
        to = peer(d)
        lane = pl.multiple_of((to * 2 + h) * kvw, kvw)
        return pltpu.make_async_remote_copy(
            src_ref=q_ref.at[0, :, pl.ds(lane, kvw)],
            dst_ref=qbuf.at[h, x],
            send_sem=q_ssem.at[d - 1, h],
            recv_sem=q_rsem.at[d - 1, h],
            device_id={"seq": to * zn + z},
            device_id_type=MESH,
        )

    def q_own(h):
        lane = pl.multiple_of((x * 2 + h) * kvw, kvw)
        return pltpu.make_async_copy(
            q_ref.at[0, :, pl.ds(lane, kvw)], qbuf.at[h, x], q_lsem.at[h]
        )

    def o_copy(d, h):
        to = peer(d)
        lane = pl.multiple_of((x * 2 + h) * kvw, kvw)
        return pltpu.make_async_remote_copy(
            src_ref=obuf.at[h, to],
            dst_ref=o_ref.at[0, :, pl.ds(lane, kvw)],
            send_sem=o_ssem.at[d - 1, h],
            recv_sem=o_rsem.at[d - 1, h],
            device_id={"seq": to * zn + z},
            device_id_type=MESH,
        )

    def o_own(h):
        lane = pl.multiple_of((x * 2 + h) * kvw, kvw)
        return pltpu.make_async_copy(
            obuf.at[h, x], o_ref.at[0, :, pl.ds(lane, kvw)], o_lsem.at[h]
        )

    def right(h, half, s):
        block = kvbuf.at[h, half, (z + zn - s) % zn]
        return pltpu.make_async_remote_copy(
            src_ref=block, dst_ref=block,
            send_sem=rt_ssem.at[h, half, s], recv_sem=rt_rsem.at[h, half, s],
            device_id={"seq": up}, device_id_type=MESH,
        )

    def left(h, half, s):
        block = kvbuf.at[h, half, (z + s) % zn]
        return pltpu.make_async_remote_copy(
            src_ref=block, dst_ref=block,
            send_sem=lf_ssem.at[h, half, s], recv_sem=lf_rsem.at[h, half, s],
            device_id={"seq": down}, device_id_type=MESH,
        )

    for h in range(2):
        for d in range(1, XN):
            for which in range(2):
                kv_copy(d, h, which).start()
        for which in range(2):
            kv_own(h, which).start()
    for h in range(2):
        for d in range(1, XN):
            q_copy(d, h).start()
        q_own(h).start()

    def start_ring(h):
        for d in range(1, XN):
            for which in range(2):
                kv_copy(d, h, which).wait_recv()
        for which in range(2):
            kv_own(h, which).wait()
        for half in range(2):
            right(h, half, 0).start()
            left(h, half, 0).start()

    def wait_queries(h):
        for d in range(1, XN):
            q_copy(d, h).wait_recv()
        q_own(h).wait()

    lengths = len_ref[pl.ds(dp, 1), :].astype(jnp.float32)
    docs = lengths.shape[1]
    before = (
        lax.broadcasted_iota(jnp.int32, (docs, docs), 0)
        <= lax.broadcasted_iota(jnp.int32, (docs, docs), 1)
    ).astype(jnp.float32)
    ends = lax.dot_general(
        jnp.broadcast_to(lengths, (8, docs)), before, (((1,), (0,)), ((), ())),
        precision=lax.Precision.HIGHEST, preferred_element_type=jnp.float32,
    )[0:1, :]
    ends = jnp.broadcast_to(ends, (tok, docs))

    def first_position(r):
        return (r * zn + z) * tok

    def find_starts():
        for r in range(XN):
            positions = (
                first_position(r) + lax.broadcasted_iota(jnp.int32, (tok, docs), 0)
            ).astype(jnp.float32)
            first = jnp.max(jnp.where(ends <= positions, ends, 0.0), axis=1, keepdims=True)
            starts[r] = jnp.broadcast_to(first.astype(jnp.int32), (tok, HD))

    def bias_of(r, blocks):
        q_pos = first_position(r) + lax.broadcasted_iota(jnp.int32, (tok, HD), 0)
        first = starts[r]
        lane = lax.broadcasted_iota(jnp.int32, (tok, HD), 1)
        parts = []
        for i in range(0, len(blocks), 2):
            (ra, za), (rb, zb) = blocks[i], blocks[i + 1]
            base_a, base_b = (ra * zn + za) * tok, (rb * zn + zb) * tok - tok
            k_pos = jnp.where(lane < tok, base_a, base_b) + lane
            ok = (k_pos >= first) & (k_pos <= q_pos)
            parts.append(jnp.where(ok, 0.0, NEG).astype(jnp.float32))
        return parts

    heads_tile = 4

    def update(h, half, r, zs, only_first, fresh):
        rows = [0] if only_first else [0, 1]
        blocks = [(2 * half + k, zb) for zb in zs for k in rows]
        bias = bias_of(r, blocks)
        keys = jnp.concatenate([kvbuf[h, half, zb, 0, k] for zb in zs for k in rows], axis=0)
        vals = jnp.concatenate([kvbuf[h, half, zb, 1, k] for zb in zs for k in rows], axis=0)
        groups = len(bias)
        rows_tile = heads_tile * tok

        def tile(j, carry):
            lanes = pl.multiple_of(j * heads_tile * HD, heads_tile * HD)
            at = pl.ds(pl.multiple_of(j * rows_tile, rows_tile), rows_tile)
            q = qbuf[h, r, :, pl.ds(lanes, heads_tile * HD)]
            q = jnp.concatenate([q[:, i * HD:(i + 1) * HD] for i in range(heads_tile)], axis=0)
            s = lax.dot_general(
                q, keys, (((1,), (1,)), ((), ())), preferred_element_type=jnp.float32
            )
            parts = [
                (s[:, g * HD:(g + 1) * HD].reshape(heads_tile, tok, HD) * scale2 + bias[g][None])
                .reshape(rows_tile, HD)
                for g in range(groups)
            ]
            top = functools.reduce(jnp.maximum, parts)
            top = jnp.max(top, axis=1, keepdims=True)
            if fresh:
                m_new = jnp.broadcast_to(top, (rows_tile, HD))
            else:
                m_old = mx[r, at, :]
                m_new = jnp.maximum(m_old, top)
            w = [jnp.exp2(p - m_new).astype(jnp.bfloat16) for p in parts]
            part_sum = functools.reduce(jnp.add, [p.astype(jnp.float32) for p in w])
            prod = jnp.dot(
                jnp.concatenate(w, axis=1), vals, preferred_element_type=jnp.float32
            )
            if fresh:
                acc[r, at, :] = prod
                sm[r, at, :] = part_sum
            else:
                alpha = jnp.exp2(m_old - m_new)
                acc[r, at, :] = acc[r, at, :] * alpha + prod
                sm[r, at, :] = sm[r, at, :] * alpha + part_sum
            mx[r, at, :] = m_new
            return carry

        lax.fori_loop(0, GROUP // heads_tile, tile, 0)

    def work(h, half, zs, seen, fresh=False):
        update(h, half, 2 * half + 1, zs, False, fresh)
        single = len(zs) == 1

        if seen is None:
            update(h, half, 2 * half, zs, not single, fresh)
        else:
            @pl.when(seen)
            def _():
                update(h, half, 2 * half, zs, not single, fresh)
        if half == 0:
            @pl.when(z == 0)
            def _():
                update(h, 0, 2, zs, False, False)

    def finish(h):
        for d in (2, 1, 3, 0):
            r = peer(d)
            for i in range(GROUP):
                at = pl.ds(i * tok, tok)
                total = jnp.sum(sm[r, at, :], axis=1, keepdims=True)
                obuf[h, r, :, i * HD:(i + 1) * HD] = (acc[r, at, :] / total).astype(jnp.bfloat16)
            if d:
                o_copy(d, h).start()
            else:
                o_own(h).start()

    right_steps = (half_ring, half_ring - 1)
    left_steps = (half_ring - 1, half_ring)

    def forward_pair(h, s):
        for half in range(2):
            right(h, half, s - 1).wait_recv()
            if right_steps[half] == half_ring:
                right(h, half, s).start()
            else:
                @pl.when(s < half_ring - 1)
                def _():
                    right(h, half, s).start()
            left(h, half, s - 1).wait_recv()
            if left_steps[half] == half_ring:
                left(h, half, s).start()
            else:
                @pl.when(s < half_ring - 1)
                def _():
                    left(h, half, s).start()

    def work_pair(h, s):
        zs = [(z + zn - s) % zn, (z + s) % zn]
        seen = (z >= s) | (z + s >= zn)
        for half in (1, 0):
            work(h, half, zs, seen)

    start_ring(0)
    find_starts()
    for h in range(2):
        if h == 0:
            forward_pair(h, 1)
            wait_queries(h)
        else:
            wait_queries(h)
        for half in (1, 0):
            work(h, half, [z], None, fresh=True)
        if h == 1:
            forward_pair(h, 1)
        work_pair(h, 1)

        def step(s, carry):
            forward_pair(h, s)
            work_pair(h, s)
            return carry

        lax.fori_loop(2, half_ring, step, 0)
        if h == 0:
            start_ring(1)
        right(h, 0, half_ring - 1).wait_recv()
        left(h, 1, half_ring - 1).wait_recv()
        far = (z + half_ring) % zn
        for half in (1, 0):
            work(h, half, [far], z >= half_ring)
        finish(h)

    for h in range(2):
        for d in range(1, XN):
            o_copy(d, h).wait()
            q_copy(d, h).wait_send()
            for which in range(2):
                kv_copy(d, h, which).wait_send()
        o_own(h).wait()
        for half in range(2):
            def drain_right(s, carry):
                right(h, half, s).wait_send()
                return carry

            def drain_left(s, carry):
                left(h, half, s).wait_send()
                return carry

            lax.fori_loop(0, right_steps[half], drain_right, 0)
            lax.fori_loop(0, left_steps[half], drain_left, 0)


def per_device(queries, keys, values, doc_lengths):
    tok = queries.shape[1]
    zn = lax.axis_size("seq") // XN
    dma, vmem = pltpu.SemaphoreType.DMA, pltpu.VMEM
    kvw = GROUP * HD
    return pl.pallas_call(
        functools.partial(kernel, zn, tok),
        out_shape=jax.ShapeDtypeStruct(queries.shape, jnp.bfloat16),
        in_specs=[pl.BlockSpec(memory_space=pltpu.VMEM)] * 4,
        out_specs=pl.BlockSpec(memory_space=pltpu.VMEM),
        scratch_shapes=[
            vmem((2, XN, tok, kvw), jnp.bfloat16),
            vmem((2, 2, zn, 2, 2, tok, HD), jnp.bfloat16),
            vmem((2, XN, tok, kvw), jnp.bfloat16),
            vmem((XN, GROUP * tok, HD), jnp.float32),
            vmem((XN, GROUP * tok, HD), jnp.float32),
            vmem((XN, GROUP * tok, HD), jnp.float32),
            vmem((XN, tok, HD), jnp.int32),
            dma((XN - 1, 2, 2)), dma((XN - 1, 2, 2)), dma((2, 2)),
            dma((XN - 1, 2)), dma((XN - 1, 2)), dma((2,)),
            dma((2, 2, zn // 2)), dma((2, 2, zn // 2)),
            dma((2, 2, zn // 2)), dma((2, 2, zn // 2)),
            dma((XN - 1, 2)), dma((XN - 1, 2)), dma((2,)),
        ],
        compiler_params=pltpu.CompilerParams(collective_id=0, has_side_effects=True),
        name="ring_attention",
    )(queries, keys, values, doc_lengths)


def solution(mesh):
    placed = (P("dp", "seq", None), P("dp", "seq", None), P("dp", "seq", None), P())
    return jax.shard_map(
        per_device, mesh=mesh, in_specs=placed, out_specs=P("dp", "seq", None), check_vma=False
    )
```

```python
import functools
import math

import jax
import jax.numpy as jnp
from jax import lax
from jax.experimental import pallas as pl
from jax.experimental.pallas import tpu as pltpu
from jax.sharding import PartitionSpec as P

QH = 64
KVH = 8
HD = 128
GROUP = 8
XN = 4
NEG = -1e30
SUMS = 16
MESH = pl.DeviceIdType.MESH


def kernel(
    zn, tok, q_ref, k_ref, v_ref, len_ref, o_ref,
    qbuf, kvbuf, obuf, acc, mx, starts,
    kv_ssem, kv_rsem, kv_lsem, q_ssem, q_rsem, q_lsem,
    rt_ssem, rt_rsem, lf_ssem, lf_rsem, o_ssem, o_rsem, o_lsem,
):
    me = lax.axis_index("seq")
    x, z = me // zn, me % zn
    dp = lax.axis_index("dp")
    up = x * zn + (z + 1) % zn
    down = x * zn + (z + zn - 1) % zn
    scale2 = math.log2(math.e) / math.sqrt(HD)
    half_ring = zn // 2
    kvw = GROUP * HD

    def peer(d):
        return (x + d) % XN

    barrier = pltpu.get_barrier_semaphore()
    for other in [up, down] + [peer(d) * zn + z for d in range(1, XN)]:
        pl.semaphore_signal(barrier, inc=1, device_id={"seq": other}, device_id_type=MESH)
    pl.semaphore_wait(barrier, XN + 1)

    def kv_copy(d, h, which):
        src = (k_ref, v_ref)[which]
        to = peer(d)
        lane = pl.multiple_of((to * 2 + h) * HD, HD)
        return pltpu.make_async_remote_copy(
            src_ref=src.at[0, :, pl.ds(lane, HD)],
            dst_ref=kvbuf.at[h, x // 2, z, which, x % 2],
            send_sem=kv_ssem.at[d - 1, h, which],
            recv_sem=kv_rsem.at[d - 1, h, which],
            device_id={"seq": to * zn + z},
            device_id_type=MESH,
        )

    def kv_own(h, which):
        src = (k_ref, v_ref)[which]
        lane = pl.multiple_of((x * 2 + h) * HD, HD)
        return pltpu.make_async_copy(
            src.at[0, :, pl.ds(lane, HD)],
            kvbuf.at[h, x // 2, z, which, x % 2],
            kv_lsem.at[h, which],
        )

    def q_copy(d, h):
        to = peer(d)
        lane = pl.multiple_of((to * 2 + h) * kvw, kvw)
        return pltpu.make_async_remote_copy(
            src_ref=q_ref.at[0, :, pl.ds(lane, kvw)],
            dst_ref=qbuf.at[h, x],
            send_sem=q_ssem.at[d - 1, h],
            recv_sem=q_rsem.at[d - 1, h],
            device_id={"seq": to * zn + z},
            device_id_type=MESH,
        )

    def q_own(h):
        lane = pl.multiple_of((x * 2 + h) * kvw, kvw)
        return pltpu.make_async_copy(
            q_ref.at[0, :, pl.ds(lane, kvw)], qbuf.at[h, x], q_lsem.at[h]
        )

    def o_copy(d, h):
        to = peer(d)
        lane = pl.multiple_of((x * 2 + h) * kvw, kvw)
        return pltpu.make_async_remote_copy(
            src_ref=obuf.at[h, to],
            dst_ref=o_ref.at[0, :, pl.ds(lane, kvw)],
            send_sem=o_ssem.at[d - 1, h],
            recv_sem=o_rsem.at[d - 1, h],
            device_id={"seq": to * zn + z},
            device_id_type=MESH,
        )

    def o_own(h):
        lane = pl.multiple_of((x * 2 + h) * kvw, kvw)
        return pltpu.make_async_copy(
            obuf.at[h, x], o_ref.at[0, :, pl.ds(lane, kvw)], o_lsem.at[h]
        )

    def right(h, half, s):
        block = kvbuf.at[h, half, (z + zn - s) % zn]
        return pltpu.make_async_remote_copy(
            src_ref=block, dst_ref=block,
            send_sem=rt_ssem.at[h, half, s], recv_sem=rt_rsem.at[h, half, s],
            device_id={"seq": up}, device_id_type=MESH,
        )

    def left(h, half, s):
        block = kvbuf.at[h, half, (z + s) % zn]
        return pltpu.make_async_remote_copy(
            src_ref=block, dst_ref=block,
            send_sem=lf_ssem.at[h, half, s], recv_sem=lf_rsem.at[h, half, s],
            device_id={"seq": down}, device_id_type=MESH,
        )

    for h in range(2):
        for d in range(1, XN):
            for which in range(2):
                kv_copy(d, h, which).start()
        for which in range(2):
            kv_own(h, which).start()
    for h in range(2):
        for d in range(1, XN):
            q_copy(d, h).start()
        q_own(h).start()

    def start_ring(h):
        for d in range(1, XN):
            for which in range(2):
                kv_copy(d, h, which).wait_recv()
        for which in range(2):
            kv_own(h, which).wait()
        for half in range(2):
            right(h, half, 0).start()
            left(h, half, 0).start()

    def wait_queries(h):
        for d in range(1, XN):
            q_copy(d, h).wait_recv()
        q_own(h).wait()

    lengths = len_ref[pl.ds(dp, 1), :].astype(jnp.float32)
    docs = lengths.shape[1]
    before = (
        lax.broadcasted_iota(jnp.int32, (docs, docs), 1)
        <= lax.broadcasted_iota(jnp.int32, (docs, docs), 0)
    ).astype(jnp.float32)

    def first_position(r):
        return (r * zn + z) * tok

    def token_row(rows):
        lane = lax.broadcasted_iota(jnp.int32, (rows, 2 * tok), 1)
        return jnp.where(lane < tok, lane, lane - tok)

    def find_starts():
        ends = jnp.sum(before * lengths, axis=1, keepdims=True)
        ends = jnp.broadcast_to(ends, (docs, 2 * tok))
        for r in range(XN):
            positions = (first_position(r) + token_row(docs)).astype(jnp.float32)
            first = jnp.max(jnp.where(ends <= positions, ends, 0.0), axis=0, keepdims=True)
            starts[r] = jnp.broadcast_to(first.astype(jnp.int32), (8, 2 * tok))

    def bias_of(r, blocks):
        q_pos = first_position(r) + token_row(tok)
        first = jnp.broadcast_to(starts[r][0:1, :], (tok, 2 * tok))
        key = lax.broadcasted_iota(jnp.int32, (tok, 2 * tok), 0)
        parts = []
        for rk, zk in blocks:
            k_pos = (rk * zn + zk) * tok + key
            ok = (k_pos >= first) & (k_pos <= q_pos)
            parts.append(jnp.where(ok, 0.0, NEG).astype(jnp.float32))
        return jnp.concatenate(parts, axis=0)

    heads_tile = 4
    cols = heads_tile * tok

    def update(h, half, r, zs, only_first, fresh):
        rows = [0] if only_first else [0, 1]
        bias = bias_of(r, [(2 * half + k, zb) for zb in zs for k in rows])
        keys = jnp.concatenate([kvbuf[h, half, zb, 0, k] for zb in zs for k in rows], axis=0)
        vals = jnp.concatenate([kvbuf[h, half, zb, 1, k] for zb in zs for k in rows], axis=0)
        count = keys.shape[0]
        vals = jnp.concatenate([vals.T, jnp.ones((SUMS, count), jnp.bfloat16)], axis=0)
        for j in range(GROUP // heads_tile):
            q = qbuf[h, r, :, j * heads_tile * HD:(j + 1) * heads_tile * HD]
            q = jnp.concatenate([q[:, i * HD:(i + 1) * HD] for i in range(heads_tile)], axis=0)
            at = slice(j * cols, (j + 1) * cols)
            s = lax.dot_general(
                keys, q, (((1,), (1,)), ((), ())), preferred_element_type=jnp.float32
            )
            s = s * scale2 + jnp.concatenate([bias] * (heads_tile // 2), axis=1)
            m_new = jnp.max(s, axis=0, keepdims=True)
            if not fresh:
                m_old = mx[h, r, 0:1, at]
                m_new = jnp.maximum(m_old, m_new)
            w = jnp.exp2(s - m_new).astype(jnp.bfloat16)
            prod = jnp.dot(vals, w, preferred_element_type=jnp.float32)
            if not fresh:
                prod = acc[h, r, :, at] * jnp.exp2(m_old - m_new) + prod
            acc[h, r, :, at] = prod
            mx[h, r, 0:1, at] = m_new

    def work(h, half, zs, seen, fresh=False):
        update(h, half, 2 * half + 1, zs, False, fresh)
        single = len(zs) == 1

        if seen is None:
            update(h, half, 2 * half, zs, not single, fresh)
        else:
            @pl.when(seen)
            def _():
                update(h, half, 2 * half, zs, not single, fresh)
        if half == 0:
            @pl.when(z == 0)
            def _():
                update(h, 0, 2, zs, False, False)

    def finish(h):
        def one(r):
            o = acc[h, r, :HD, :] / acc[h, r, HD:HD + 1, :]
            for i in range(GROUP):
                obuf[h, r, :, i * HD:(i + 1) * HD] = (
                    o[:, i * tok:(i + 1) * tok].T.astype(jnp.bfloat16)
                )

        for d in (2, 1, 3, 0):
            one(peer(d))
            if d:
                o_copy(d, h).start()
            else:
                o_own(h).start()

    right_steps = (half_ring, half_ring - 1)
    left_steps = (half_ring - 1, half_ring)

    def forward(h, half, s):
        for copy, steps in ((right, right_steps), (left, left_steps)):
            copy(h, half, s - 1).wait_recv()
            if steps[half] == half_ring:
                copy(h, half, s).start()
            else:
                @pl.when(s < half_ring - 1)
                def _():
                    copy(h, half, s).start()

    def over_heads(body):
        lax.fori_loop(0, 2, lambda h, carry: (body(h), carry)[1], 0)

    def work_pair(h, half, s):
        work(h, half, [(z + zn - s) % zn, (z + s) % zn], (z >= s) | (z + s >= zn))

    start_ring(0)
    start_ring(1)
    find_starts()
    for h in range(2):
        for half in (1, 0):
            forward(h, half, 1)
    for h in range(2):
        wait_queries(h)

    def first_step(h):
        for half in (1, 0):
            work(h, half, [z], None, fresh=True)
        for half in (1, 0):
            work_pair(h, half, 1)

    over_heads(first_step)

    def step(s, carry):
        def heads(h):
            for half in (1, 0):
                forward(h, half, s)
                work_pair(h, half, s)

        over_heads(heads)
        return carry

    lax.fori_loop(2, half_ring, step, 0)
    far = (z + half_ring) % zn

    for h in range(2):
        for half in (1, 0):
            (right if half == 0 else left)(h, half, half_ring - 1).wait_recv()
            work(h, half, [far], z >= half_ring)
        finish(h)

    for h in range(2):
        for d in range(1, XN):
            o_copy(d, h).wait()
            q_copy(d, h).wait_send()
            for which in range(2):
                kv_copy(d, h, which).wait_send()
        o_own(h).wait()
        for half in range(2):
            def drain_right(s, carry):
                right(h, half, s).wait_send()
                return carry

            def drain_left(s, carry):
                left(h, half, s).wait_send()
                return carry

            lax.fori_loop(0, right_steps[half], drain_right, 0)
            lax.fori_loop(0, left_steps[half], drain_left, 0)


def per_device(queries, keys, values, doc_lengths):
    tok = queries.shape[1]
    zn = lax.axis_size("seq") // XN
    dma, vmem = pltpu.SemaphoreType.DMA, pltpu.VMEM
    kvw = GROUP * HD
    return pl.pallas_call(
        functools.partial(kernel, zn, tok),
        out_shape=jax.ShapeDtypeStruct(queries.shape, jnp.bfloat16),
        in_specs=[pl.BlockSpec(memory_space=pltpu.VMEM)] * 4,
        out_specs=pl.BlockSpec(memory_space=pltpu.VMEM),
        scratch_shapes=[
            vmem((2, XN, tok, kvw), jnp.bfloat16),
            vmem((2, 2, zn, 2, 2, tok, HD), jnp.bfloat16),
            vmem((2, XN, tok, kvw), jnp.bfloat16),
            vmem((2, XN, HD + SUMS, GROUP * tok), jnp.float32),
            vmem((2, XN, 8, GROUP * tok), jnp.float32),
            vmem((XN, 8, 2 * tok), jnp.int32),
            dma((XN - 1, 2, 2)), dma((XN - 1, 2, 2)), dma((2, 2)),
            dma((XN - 1, 2)), dma((XN - 1, 2)), dma((2,)),
            dma((2, 2, zn // 2)), dma((2, 2, zn // 2)),
            dma((2, 2, zn // 2)), dma((2, 2, zn // 2)),
            dma((XN - 1, 2)), dma((XN - 1, 2)), dma((2,)),
        ],
        compiler_params=pltpu.CompilerParams(collective_id=0, has_side_effects=True),
        name="ring_attention",
    )(queries, keys, values, doc_lengths)


def solution(mesh):
    placed = (P("dp", "seq", None), P("dp", "seq", None), P("dp", "seq", None), P())
    return jax.shard_map(
        per_device, mesh=mesh, in_specs=placed, out_specs=P("dp", "seq", None), check_vma=False
    )
```

```python
import functools
import math

import jax
import jax.numpy as jnp
from jax import lax
from jax.experimental import pallas as pl
from jax.experimental.pallas import tpu as pltpu
from jax.sharding import PartitionSpec as P

QH = 64
KVH = 8
HD = 128
GROUP = 8
XN = 4
NEG = -1e30
SUMS = 16
MESH = pl.DeviceIdType.MESH


def kernel(
    zn, tok, q_ref, k_ref, v_ref, len_ref, o_ref,
    qbuf, kvbuf, obuf, acc, mx, starts,
    kv_ssem, kv_rsem, kv_lsem, q_ssem, q_rsem, q_lsem,
    rt_ssem, rt_rsem, lf_ssem, lf_rsem, o_ssem, o_rsem, o_lsem,
):
    me = lax.axis_index("seq")
    x, z = me // zn, me % zn
    dp = lax.axis_index("dp")
    up = x * zn + (z + 1) % zn
    down = x * zn + (z + zn - 1) % zn
    scale2 = math.log2(math.e) / math.sqrt(HD)
    half_ring = zn // 2
    kvw = GROUP * HD

    def peer(d):
        return (x + d) % XN

    barrier = pltpu.get_barrier_semaphore()
    for other in [up, down] + [peer(d) * zn + z for d in range(1, XN)]:
        pl.semaphore_signal(barrier, inc=1, device_id={"seq": other}, device_id_type=MESH)
    pl.semaphore_wait(barrier, XN + 1)

    def kv_copy(d, h, which):
        src = (k_ref, v_ref)[which]
        to = peer(d)
        lane = pl.multiple_of((to * 2 + h) * HD, HD)
        return pltpu.make_async_remote_copy(
            src_ref=src.at[0, :, pl.ds(lane, HD)],
            dst_ref=kvbuf.at[h, x // 2, z, which, x % 2],
            send_sem=kv_ssem.at[d - 1, h, which],
            recv_sem=kv_rsem.at[d - 1, h, which],
            device_id={"seq": to * zn + z},
            device_id_type=MESH,
        )

    def kv_own(h, which):
        src = (k_ref, v_ref)[which]
        lane = pl.multiple_of((x * 2 + h) * HD, HD)
        return pltpu.make_async_copy(
            src.at[0, :, pl.ds(lane, HD)],
            kvbuf.at[h, x // 2, z, which, x % 2],
            kv_lsem.at[h, which],
        )

    def q_copy(d, h):
        to = peer(d)
        lane = pl.multiple_of((to * 2 + h) * kvw, kvw)
        return pltpu.make_async_remote_copy(
            src_ref=q_ref.at[0, :, pl.ds(lane, kvw)],
            dst_ref=qbuf.at[h, x],
            send_sem=q_ssem.at[d - 1, h],
            recv_sem=q_rsem.at[d - 1, h],
            device_id={"seq": to * zn + z},
            device_id_type=MESH,
        )

    def q_own(h):
        lane = pl.multiple_of((x * 2 + h) * kvw, kvw)
        return pltpu.make_async_copy(
            q_ref.at[0, :, pl.ds(lane, kvw)], qbuf.at[h, x], q_lsem.at[h]
        )

    def o_copy(d, h):
        to = peer(d)
        lane = pl.multiple_of((x * 2 + h) * kvw, kvw)
        return pltpu.make_async_remote_copy(
            src_ref=obuf.at[h, to],
            dst_ref=o_ref.at[0, :, pl.ds(lane, kvw)],
            send_sem=o_ssem.at[d - 1, h],
            recv_sem=o_rsem.at[d - 1, h],
            device_id={"seq": to * zn + z},
            device_id_type=MESH,
        )

    def o_own(h):
        lane = pl.multiple_of((x * 2 + h) * kvw, kvw)
        return pltpu.make_async_copy(
            obuf.at[h, x], o_ref.at[0, :, pl.ds(lane, kvw)], o_lsem.at[h]
        )

    def right(h, half, s):
        block = kvbuf.at[h, half, (z + zn - s) % zn]
        return pltpu.make_async_remote_copy(
            src_ref=block, dst_ref=block,
            send_sem=rt_ssem.at[h, half, s], recv_sem=rt_rsem.at[h, half, s],
            device_id={"seq": up}, device_id_type=MESH,
        )

    def left(h, half, s):
        block = kvbuf.at[h, half, (z + s) % zn]
        return pltpu.make_async_remote_copy(
            src_ref=block, dst_ref=block,
            send_sem=lf_ssem.at[h, half, s], recv_sem=lf_rsem.at[h, half, s],
            device_id={"seq": down}, device_id_type=MESH,
        )

    for h in range(2):
        for d in range(1, XN):
            for which in range(2):
                kv_copy(d, h, which).start()
        for which in range(2):
            kv_own(h, which).start()
    def start_ring(h):
        for d in range(1, XN):
            for which in range(2):
                kv_copy(d, h, which).wait_recv()
        for which in range(2):
            kv_own(h, which).wait()
        for half in range(2):
            right(h, half, 0).start()
            left(h, half, 0).start()

    def wait_queries(h):
        for d in range(1, XN):
            q_copy(d, h).wait_recv()
        q_own(h).wait()

    lengths = len_ref[pl.ds(dp, 1), :].astype(jnp.float32)
    docs = lengths.shape[1]
    before = (
        lax.broadcasted_iota(jnp.int32, (docs, docs), 1)
        <= lax.broadcasted_iota(jnp.int32, (docs, docs), 0)
    ).astype(jnp.float32)

    def first_position(r):
        return (r * zn + z) * tok

    def token_row(rows):
        lane = lax.broadcasted_iota(jnp.int32, (rows, 2 * tok), 1)
        return jnp.where(lane < tok, lane, lane - tok)

    def find_starts():
        ends = jnp.sum(before * lengths, axis=1, keepdims=True)
        ends = jnp.broadcast_to(ends, (docs, 2 * tok))
        for r in range(XN):
            positions = (first_position(r) + token_row(docs)).astype(jnp.float32)
            first = jnp.max(jnp.where(ends <= positions, ends, 0.0), axis=0, keepdims=True)
            starts[r] = jnp.broadcast_to(first.astype(jnp.int32), (8, 2 * tok))

    def bias_of(r, blocks):
        q_pos = first_position(r) + token_row(tok)
        first = jnp.broadcast_to(starts[r][0:1, :], (tok, 2 * tok))
        key = lax.broadcasted_iota(jnp.int32, (tok, 2 * tok), 0)
        parts = []
        for rk, zk in blocks:
            k_pos = (rk * zn + zk) * tok + key
            ok = (k_pos >= first) & (k_pos <= q_pos)
            parts.append(jnp.where(ok, 0.0, NEG).astype(jnp.float32))
        return jnp.concatenate(parts, axis=0)

    heads_tile = 4
    cols = heads_tile * tok

    def update(h, half, rows, zs, fresh):
        order = [(k, zb) for k in range(2) for zb in zs]
        keys = jnp.concatenate([kvbuf[h, half, zb, 0, k] for k, zb in order], axis=0)
        vals = jnp.concatenate([kvbuf[h, half, zb, 1, k] for k, zb in order], axis=0)
        vals = jnp.concatenate([vals.T, jnp.ones((SUMS, vals.shape[0]), jnp.bfloat16)], axis=0)
        tiles = []
        for r, only_first in rows:
            blocks = order[:len(zs)] if only_first else order
            bias = bias_of(r, [(2 * half + k, zb) for k, zb in blocks])
            bias = jnp.concatenate([bias] * (heads_tile // 2), axis=1)
            for j in range(GROUP // heads_tile):
                tiles.append((r, bias, slice(j * cols, (j + 1) * cols), j * heads_tile * HD))

        def score(tile):
            r, bias, _, lane = tile
            q = qbuf[h, r, :, lane:lane + heads_tile * HD]
            q = jnp.concatenate([q[:, i * HD:(i + 1) * HD] for i in range(heads_tile)], axis=0)
            return lax.dot_general(
                keys[:bias.shape[0]], q, (((1,), (1,)), ((), ())),
                preferred_element_type=jnp.float32,
            )

        old = [None if fresh else mx[h, r, 0:1, at] for r, _, at, _ in tiles]
        tops, prods = [], []
        ahead = [score(tiles[0])]
        for i, (r, bias, at, _) in enumerate(tiles):
            if i + 1 < len(tiles):
                ahead.append(score(tiles[i + 1]))
            s = ahead[i] * scale2 + bias
            top = jnp.max(s, axis=0, keepdims=True)
            if not fresh:
                top = jnp.maximum(old[i], top)
            w = jnp.exp2(s - top).astype(jnp.bfloat16)
            prods.append(
                jnp.dot(vals[:, :bias.shape[0]], w, preferred_element_type=jnp.float32)
            )
            tops.append(top)
        for i, (r, _, at, _) in enumerate(tiles):
            if fresh:
                acc[h, r, :, at] = prods[i]
            else:
                acc[h, r, :, at] = acc[h, r, :, at] * jnp.exp2(old[i] - tops[i]) + prods[i]
            mx[h, r, 0:1, at] = tops[i]

    def work(h, half, zs, fresh=False):
        single = len(zs) == 1
        second, first = (2 * half + 1, False), (2 * half, not single)
        crossing = (2, False)
        if half == 1:
            update(h, half, [second, first], zs, fresh)
        elif fresh:
            update(h, half, [second, first], zs, fresh)

            @pl.when(z == 0)
            def _():
                update(h, half, [crossing], zs, False)
        else:
            @pl.when(z == 0)
            def _():
                update(h, half, [second, crossing], zs, fresh)

            @pl.when(z != 0)
            def _():
                update(h, half, [second, first], zs, fresh)

    def finish(h):
        def one(r):
            o = acc[h, r, :HD, :] / acc[h, r, HD:HD + 1, :]
            for i in range(GROUP):
                obuf[h, r, :, i * HD:(i + 1) * HD] = (
                    o[:, i * tok:(i + 1) * tok].T.astype(jnp.bfloat16)
                )

        for d in (2, 1, 3, 0):
            one(peer(d))
            if d:
                o_copy(d, h).start()
            else:
                o_own(h).start()

    right_steps = (half_ring, half_ring - 1)
    left_steps = (half_ring - 1, half_ring)

    def forward(h, half, s):
        for copy, steps in ((right, right_steps), (left, left_steps)):
            copy(h, half, s - 1).wait_recv()
            if steps[half] == half_ring:
                copy(h, half, s).start()
            else:
                @pl.when(s < half_ring - 1)
                def _():
                    copy(h, half, s).start()

    def over_heads(body):
        lax.fori_loop(0, 2, lambda h, carry: (body(h), carry)[1], 0)

    def work_pair(h, half, s):
        work(h, half, [(z + zn - s) % zn, (z + s) % zn])

    start_ring(0)
    start_ring(1)
    for h in range(2):
        for d in range(1, XN):
            q_copy(d, h).start()
        q_own(h).start()
    find_starts()
    for h in range(2):
        for half in (1, 0):
            forward(h, half, 1)
    for h in range(2):
        wait_queries(h)
        for half in (1, 0):
            work(h, half, [z], fresh=True)

    def pair_step(h, half, s):
        @pl.when(s < half_ring - 1)
        def _():
            forward(h, half, s + 1)

        work_pair(h, half, s)

    def step(s, carry):
        def heads(h, carry):
            for half in (1, 0):
                pair_step(h, half, s)
            return carry

        return lax.fori_loop(0, 2, heads, carry)

    lax.fori_loop(1, half_ring, step, 0)
    far = (z + half_ring) % zn

    def drain(h, begin, end):
        for copy, steps in ((right, right_steps), (left, left_steps)):
            for half in range(2):
                def wait_one(s, carry):
                    copy(h, half, s).wait_send()
                    return carry

                lax.fori_loop(begin, end or steps[half], wait_one, 0)

    for h in range(2):
        drain(h, 0, half_ring - 1)
        for d in range(1, XN):
            q_copy(d, h).wait_send()
            for which in range(2):
                kv_copy(d, h, which).wait_send()
    for h in range(2):
        for half in (1, 0):
            (right if half == 0 else left)(h, half, half_ring - 1).wait_recv()
            work(h, half, [far])
        finish(h)
    for h in range(2):
        drain(h, half_ring - 1, None)
        for d in range(1, XN):
            o_copy(d, h).wait()
        o_own(h).wait()


def per_device(queries, keys, values, doc_lengths):
    tok = queries.shape[1]
    zn = lax.axis_size("seq") // XN
    dma, vmem = pltpu.SemaphoreType.DMA, pltpu.VMEM
    kvw = GROUP * HD
    return pl.pallas_call(
        functools.partial(kernel, zn, tok),
        out_shape=jax.ShapeDtypeStruct(queries.shape, jnp.bfloat16),
        in_specs=[pl.BlockSpec(memory_space=pl.ANY)] * 3 + [pl.BlockSpec(memory_space=pltpu.VMEM)],
        out_specs=pl.BlockSpec(memory_space=pl.ANY),
        scratch_shapes=[
            vmem((2, XN, tok, kvw), jnp.bfloat16),
            vmem((2, 2, zn, 2, 2, tok, HD), jnp.bfloat16),
            vmem((2, XN, tok, kvw), jnp.bfloat16),
            vmem((2, XN, HD + SUMS, GROUP * tok), jnp.float32),
            vmem((2, XN, 8, GROUP * tok), jnp.float32),
            vmem((XN, 8, 2 * tok), jnp.int32),
            dma((XN - 1, 2, 2)), dma((XN - 1, 2, 2)), dma((2, 2)),
            dma((XN - 1, 2)), dma((XN - 1, 2)), dma((2,)),
            dma((2, 2, zn // 2)), dma((2, 2, zn // 2)),
            dma((2, 2, zn // 2)), dma((2, 2, zn // 2)),
            dma((XN - 1, 2)), dma((XN - 1, 2)), dma((2,)),
        ],
        compiler_params=pltpu.CompilerParams(collective_id=0, has_side_effects=True),
        name="ring_attention",
    )(queries, keys, values, doc_lengths)


def solution(mesh):
    placed = (P("dp", "seq", None), P("dp", "seq", None), P("dp", "seq", None), P())
    return jax.shard_map(
        per_device, mesh=mesh, in_specs=placed, out_specs=P("dp", "seq", None), check_vma=False
    )
```

```python
import functools
import math

import jax
import jax.numpy as jnp
from jax import lax
from jax.experimental import pallas as pl
from jax.experimental.pallas import tpu as pltpu
from jax.sharding import PartitionSpec as P

QH = 64
KVH = 8
HD = 128
GROUP = 8
XN = 4
NEG = -1e30
SUMS = 16
MESH = pl.DeviceIdType.MESH


def kernel(
    zn, tok, q_ref, k_ref, v_ref, len_ref, o_ref,
    qbuf, kvbuf, obuf, acc, mx, starts,
    kv_ssem, kv_rsem, kv_lsem, q_ssem, q_rsem, q_lsem,
    rt_ssem, rt_rsem, lf_ssem, lf_rsem, o_ssem, o_rsem, o_lsem,
):
    me = lax.axis_index("seq")
    x, z = me // zn, me % zn
    dp = lax.axis_index("dp")
    up = x * zn + (z + 1) % zn
    down = x * zn + (z + zn - 1) % zn
    scale2 = math.log2(math.e) / math.sqrt(HD)
    half_ring = zn // 2
    kvw = GROUP * HD

    def peer(d):
        return (x + d) % XN

    barrier = pltpu.get_barrier_semaphore()
    for other in [up, down] + [peer(d) * zn + z for d in range(1, XN)]:
        pl.semaphore_signal(barrier, inc=1, device_id={"seq": other}, device_id_type=MESH)
    pl.semaphore_wait(barrier, XN + 1)

    def kv_copy(d, h, which):
        src = (k_ref, v_ref)[which]
        to = peer(d)
        lane = pl.multiple_of((to * 2 + h) * HD, HD)
        return pltpu.make_async_remote_copy(
            src_ref=src.at[0, :, pl.ds(lane, HD)],
            dst_ref=kvbuf.at[h, x // 2, z, which, x % 2],
            send_sem=kv_ssem.at[d - 1, h, which],
            recv_sem=kv_rsem.at[d - 1, h, which],
            device_id={"seq": to * zn + z},
            device_id_type=MESH,
        )

    def kv_own(h, which):
        src = (k_ref, v_ref)[which]
        lane = pl.multiple_of((x * 2 + h) * HD, HD)
        return pltpu.make_async_copy(
            src.at[0, :, pl.ds(lane, HD)],
            kvbuf.at[h, x // 2, z, which, x % 2],
            kv_lsem.at[h, which],
        )

    def q_copy(d, h):
        to = peer(d)
        lane = pl.multiple_of((to * 2 + h) * kvw, kvw)
        return pltpu.make_async_remote_copy(
            src_ref=q_ref.at[0, :, pl.ds(lane, kvw)],
            dst_ref=qbuf.at[h, x],
            send_sem=q_ssem.at[d - 1, h],
            recv_sem=q_rsem.at[d - 1, h],
            device_id={"seq": to * zn + z},
            device_id_type=MESH,
        )

    def q_own(h):
        lane = pl.multiple_of((x * 2 + h) * kvw, kvw)
        return pltpu.make_async_copy(
            q_ref.at[0, :, pl.ds(lane, kvw)], qbuf.at[h, x], q_lsem.at[h]
        )

    def o_copy(d, h):
        to = peer(d)
        lane = pl.multiple_of((x * 2 + h) * kvw, kvw)
        return pltpu.make_async_remote_copy(
            src_ref=obuf.at[h, to],
            dst_ref=o_ref.at[0, :, pl.ds(lane, kvw)],
            send_sem=o_ssem.at[d - 1, h],
            recv_sem=o_rsem.at[d - 1, h],
            device_id={"seq": to * zn + z},
            device_id_type=MESH,
        )

    def o_own(h):
        lane = pl.multiple_of((x * 2 + h) * kvw, kvw)
        return pltpu.make_async_copy(
            obuf.at[h, x], o_ref.at[0, :, pl.ds(lane, kvw)], o_lsem.at[h]
        )

    def right(h, half, s):
        block = kvbuf.at[h, half, (z + zn - s) % zn]
        return pltpu.make_async_remote_copy(
            src_ref=block, dst_ref=block,
            send_sem=rt_ssem.at[h, half, s], recv_sem=rt_rsem.at[h, half, s],
            device_id={"seq": up}, device_id_type=MESH,
        )

    def left(h, half, s):
        block = kvbuf.at[h, half, (z + s) % zn]
        return pltpu.make_async_remote_copy(
            src_ref=block, dst_ref=block,
            send_sem=lf_ssem.at[h, half, s], recv_sem=lf_rsem.at[h, half, s],
            device_id={"seq": down}, device_id_type=MESH,
        )

    for h in range(2):
        for d in range(1, XN):
            for which in range(2):
                kv_copy(d, h, which).start()
        for which in range(2):
            kv_own(h, which).start()
    def start_ring(h):
        for d in range(1, XN):
            for which in range(2):
                kv_copy(d, h, which).wait_recv()
        for which in range(2):
            kv_own(h, which).wait()
        for half in range(2):
            right(h, half, 0).start()
            left(h, half, 0).start()

    def wait_queries(h):
        for d in range(1, XN):
            q_copy(d, h).wait_recv()
        q_own(h).wait()

    lengths = len_ref[pl.ds(dp, 1), :].astype(jnp.float32)
    docs = lengths.shape[1]
    before = (
        lax.broadcasted_iota(jnp.int32, (docs, docs), 1)
        <= lax.broadcasted_iota(jnp.int32, (docs, docs), 0)
    ).astype(jnp.float32)

    def first_position(r):
        return (r * zn + z) * tok

    def token_row(rows):
        lane = lax.broadcasted_iota(jnp.int32, (rows, 2 * tok), 1)
        return jnp.where(lane < tok, lane, lane - tok)

    def find_starts():
        ends = jnp.sum(before * lengths, axis=1, keepdims=True)
        ends = jnp.broadcast_to(ends, (docs, 2 * tok))
        for r in range(XN):
            positions = (first_position(r) + token_row(docs)).astype(jnp.float32)
            first = jnp.max(jnp.where(ends <= positions, ends, 0.0), axis=0, keepdims=True)
            starts[r] = jnp.broadcast_to(first.astype(jnp.int32), (8, 2 * tok))

    def bias_of(r, blocks):
        q_pos = first_position(r) + token_row(tok)
        first = jnp.broadcast_to(starts[r][0:1, :], (tok, 2 * tok))
        key = lax.broadcasted_iota(jnp.int32, (tok, 2 * tok), 0)
        parts = []
        for rk, zk in blocks:
            k_pos = (rk * zn + zk) * tok + key
            ok = (k_pos >= first) & (k_pos <= q_pos)
            parts.append(jnp.where(ok, 0.0, NEG).astype(jnp.float32))
        return jnp.concatenate(parts, axis=0)

    heads_tile = 4
    cols = heads_tile * tok

    def update(h, half, rows, zs, fresh):
        order = [(k, zb) for k in range(2) for zb in zs]
        keys = jnp.concatenate([kvbuf[h, half, zb, 0, k] for k, zb in order], axis=0)
        vals = jnp.concatenate([kvbuf[h, half, zb, 1, k] for k, zb in order], axis=0)
        vals = jnp.concatenate([vals.T, jnp.ones((SUMS, vals.shape[0]), jnp.bfloat16)], axis=0)
        tiles = []
        for r, only_first in rows:
            blocks = order[:len(zs)] if only_first else order
            bias = bias_of(r, [(2 * half + k, zb) for k, zb in blocks])
            bias = jnp.concatenate([bias] * (heads_tile // 2), axis=1)
            for j in range(GROUP // heads_tile):
                tiles.append((r, bias, slice(j * cols, (j + 1) * cols), j * heads_tile * HD))

        def score(tile):
            r, bias, _, lane = tile
            q = qbuf[h, r, :, lane:lane + heads_tile * HD]
            q = jnp.concatenate([q[:, i * HD:(i + 1) * HD] for i in range(heads_tile)], axis=0)
            return lax.dot_general(
                keys[:bias.shape[0]], q, (((1,), (1,)), ((), ())),
                preferred_element_type=jnp.float32,
            )

        old = [None if fresh else mx[h, r, 0:1, at] for r, _, at, _ in tiles]
        tops, prods = [], []
        ahead = [score(tiles[0])]
        for i, (r, bias, at, _) in enumerate(tiles):
            if i + 1 < len(tiles):
                ahead.append(score(tiles[i + 1]))
            s = ahead[i] * scale2 + bias
            top = jnp.max(s, axis=0, keepdims=True)
            if not fresh:
                top = jnp.maximum(old[i], top)
            w = jnp.exp2(s - top).astype(jnp.bfloat16)
            prods.append(
                jnp.dot(vals[:, :bias.shape[0]], w, preferred_element_type=jnp.float32)
            )
            tops.append(top)
        for i, (r, _, at, _) in enumerate(tiles):
            if fresh:
                acc[h, r, :, at] = prods[i]
            else:
                acc[h, r, :, at] = acc[h, r, :, at] * jnp.exp2(old[i] - tops[i]) + prods[i]
            mx[h, r, 0:1, at] = tops[i]

    def work(h, half, zs, fresh=False):
        single = len(zs) == 1
        second, first = (2 * half + 1, False), (2 * half, not single)
        crossing = (2, False)
        if half == 1:
            update(h, half, [second, first], zs, fresh)
        elif fresh:
            update(h, half, [second, first], zs, fresh)

            @pl.when(z == 0)
            def _():
                update(h, half, [crossing], zs, False)
        else:
            @pl.when(z == 0)
            def _():
                update(h, half, [second, crossing], zs, fresh)

            @pl.when(z != 0)
            def _():
                update(h, half, [second, first], zs, fresh)

    def finish(h, r):
        o = acc[h, r, :HD, :] / acc[h, r, HD:HD + 1, :]
        for i in range(GROUP):
            obuf[h, r, :, i * HD:(i + 1) * HD] = o[:, i * tok:(i + 1) * tok].T.astype(jnp.bfloat16)
        for d in range(XN):
            @pl.when(peer(d) == r)
            def _():
                if d:
                    o_copy(d, h).start()
                else:
                    o_own(h).start()

    right_steps = (half_ring, half_ring - 1)
    left_steps = (half_ring - 1, half_ring)

    def forward(h, half, s):
        for copy, steps in ((right, right_steps), (left, left_steps)):
            copy(h, half, s - 1).wait_recv()
            if steps[half] == half_ring:
                copy(h, half, s).start()
            else:
                @pl.when(s < half_ring - 1)
                def _():
                    copy(h, half, s).start()

    def over_heads(body):
        lax.fori_loop(0, 2, lambda h, carry: (body(h), carry)[1], 0)

    def work_pair(h, half, s):
        work(h, half, [(z + zn - s) % zn, (z + s) % zn])

    start_ring(0)
    start_ring(1)
    for h in range(2):
        for d in range(1, XN):
            q_copy(d, h).start()
        q_own(h).start()
    find_starts()
    ahead = min(2, half_ring - 1)
    for s in range(1, ahead + 1):
        for h in range(2):
            for half in range(2):
                forward(h, half, s)
    for h in range(2):
        wait_queries(h)
        for half in (1, 0):
            work(h, half, [z], fresh=True)

    def pair_step(h, half, s):
        @pl.when((s >= ahead) & (s < half_ring - 1))
        def _():
            forward(h, half, s + 1)

        work_pair(h, half, s)

    def step(s, carry):
        def heads(h, carry):
            for half in range(2):
                pair_step(h, half, s)
            return carry

        return lax.fori_loop(0, 2, heads, carry)

    lax.fori_loop(1, half_ring, step, 0)
    far = (z + half_ring) % zn

    def drain(h, begin, end):
        for copy, steps in ((right, right_steps), (left, left_steps)):
            for half in range(2):
                def wait_one(s, carry):
                    copy(h, half, s).wait_send()
                    return carry

                lax.fori_loop(begin, end or steps[half], wait_one, 0)

    for h in range(2):
        drain(h, 0, half_ring - 1)
        for d in range(1, XN):
            q_copy(d, h).wait_send()
            for which in range(2):
                kv_copy(d, h, which).wait_send()
    for h in range(2):
        for half in range(2):
            (right if half == 0 else left)(h, half, half_ring - 1).wait_recv()
            work(h, half, [far])
            for r in (2 * half + 1, 2 * half):
                finish(h, r)
    for h in range(2):
        drain(h, half_ring - 1, None)
        for d in range(1, XN):
            o_copy(d, h).wait()
        o_own(h).wait()


def per_device(queries, keys, values, doc_lengths):
    tok = queries.shape[1]
    zn = lax.axis_size("seq") // XN
    dma, vmem = pltpu.SemaphoreType.DMA, pltpu.VMEM
    kvw = GROUP * HD
    return pl.pallas_call(
        functools.partial(kernel, zn, tok),
        out_shape=jax.ShapeDtypeStruct(queries.shape, jnp.bfloat16),
        in_specs=[pl.BlockSpec(memory_space=pl.ANY)] * 3 + [pl.BlockSpec(memory_space=pltpu.VMEM)],
        out_specs=pl.BlockSpec(memory_space=pl.ANY),
        scratch_shapes=[
            vmem((2, XN, tok, kvw), jnp.bfloat16),
            vmem((2, 2, zn, 2, 2, tok, HD), jnp.bfloat16),
            vmem((2, XN, tok, kvw), jnp.bfloat16),
            vmem((2, XN, HD + SUMS, GROUP * tok), jnp.float32),
            vmem((2, XN, 8, GROUP * tok), jnp.float32),
            vmem((XN, 8, 2 * tok), jnp.int32),
            dma((XN - 1, 2, 2)), dma((XN - 1, 2, 2)), dma((2, 2)),
            dma((XN - 1, 2)), dma((XN - 1, 2)), dma((2,)),
            dma((2, 2, zn // 2)), dma((2, 2, zn // 2)),
            dma((2, 2, zn // 2)), dma((2, 2, zn // 2)),
            dma((XN - 1, 2)), dma((XN - 1, 2)), dma((2,)),
        ],
        compiler_params=pltpu.CompilerParams(collective_id=0, has_side_effects=True),
        name="ring_attention",
    )(queries, keys, values, doc_lengths)


def solution(mesh):
    placed = (P("dp", "seq", None), P("dp", "seq", None), P("dp", "seq", None), P())
    return jax.shard_map(
        per_device, mesh=mesh, in_specs=placed, out_specs=P("dp", "seq", None), check_vma=False
    )
```

```python
import functools
import math

import jax
import jax.numpy as jnp
from jax import lax
from jax.experimental import pallas as pl
from jax.experimental.pallas import tpu as pltpu
from jax.sharding import PartitionSpec as P

QH = 64
KVH = 8
HD = 128
GROUP = 8
XN = 4
NEG = -1e30
SUMS = 16
MESH = pl.DeviceIdType.MESH


def kernel(
    zn, tok, q_ref, k_ref, v_ref, len_ref, o_ref,
    qbuf, kvbuf, obuf, acc, mx, starts,
    kv_ssem, kv_rsem, kv_lsem, q_ssem, q_rsem, q_lsem,
    rt_ssem, rt_rsem, lf_ssem, lf_rsem, o_ssem, o_rsem, o_lsem,
):
    me = lax.axis_index("seq")
    x, z = me // zn, me % zn
    dp = lax.axis_index("dp")
    up = x * zn + (z + 1) % zn
    down = x * zn + (z + zn - 1) % zn
    scale2 = math.log2(math.e) / math.sqrt(HD)
    half_ring = zn // 2
    kvw = GROUP * HD

    def peer(d):
        return (x + d) % XN

    barrier = pltpu.get_barrier_semaphore()
    for other in [up, down] + [peer(d) * zn + z for d in range(1, XN)]:
        pl.semaphore_signal(barrier, inc=1, device_id={"seq": other}, device_id_type=MESH)
    pl.semaphore_wait(barrier, XN + 1)

    def kv_copy(d, h, which):
        src = (k_ref, v_ref)[which]
        to = peer(d)
        lane = pl.multiple_of((to * 2 + h) * HD, HD)
        return pltpu.make_async_remote_copy(
            src_ref=src.at[0, :, pl.ds(lane, HD)],
            dst_ref=kvbuf.at[h, x // 2, z, which, x % 2],
            send_sem=kv_ssem.at[d - 1, h, which],
            recv_sem=kv_rsem.at[d - 1, h, which],
            device_id={"seq": to * zn + z},
            device_id_type=MESH,
        )

    def kv_own(h, which):
        src = (k_ref, v_ref)[which]
        lane = pl.multiple_of((x * 2 + h) * HD, HD)
        return pltpu.make_async_copy(
            src.at[0, :, pl.ds(lane, HD)],
            kvbuf.at[h, x // 2, z, which, x % 2],
            kv_lsem.at[h, which],
        )

    def q_copy(d, h):
        to = peer(d)
        lane = pl.multiple_of((to * 2 + h) * kvw, kvw)
        return pltpu.make_async_remote_copy(
            src_ref=q_ref.at[0, :, pl.ds(lane, kvw)],
            dst_ref=qbuf.at[h, x],
            send_sem=q_ssem.at[d - 1, h],
            recv_sem=q_rsem.at[d - 1, h],
            device_id={"seq": to * zn + z},
            device_id_type=MESH,
        )

    def q_own(h):
        lane = pl.multiple_of((x * 2 + h) * kvw, kvw)
        return pltpu.make_async_copy(
            q_ref.at[0, :, pl.ds(lane, kvw)], qbuf.at[h, x], q_lsem.at[h]
        )

    def o_copy(d, h):
        to = peer(d)
        lane = pl.multiple_of((x * 2 + h) * kvw, kvw)
        return pltpu.make_async_remote_copy(
            src_ref=obuf.at[h, to],
            dst_ref=o_ref.at[0, :, pl.ds(lane, kvw)],
            send_sem=o_ssem.at[d - 1, h],
            recv_sem=o_rsem.at[d - 1, h],
            device_id={"seq": to * zn + z},
            device_id_type=MESH,
        )

    def o_own(h):
        lane = pl.multiple_of((x * 2 + h) * kvw, kvw)
        return pltpu.make_async_copy(
            obuf.at[h, x], o_ref.at[0, :, pl.ds(lane, kvw)], o_lsem.at[h]
        )

    def right(h, half, s):
        block = kvbuf.at[h, half, (z + zn - s) % zn]
        return pltpu.make_async_remote_copy(
            src_ref=block, dst_ref=block,
            send_sem=rt_ssem.at[h, half, s], recv_sem=rt_rsem.at[h, half, s],
            device_id={"seq": up}, device_id_type=MESH,
        )

    def left(h, half, s):
        block = kvbuf.at[h, half, (z + s) % zn]
        return pltpu.make_async_remote_copy(
            src_ref=block, dst_ref=block,
            send_sem=lf_ssem.at[h, half, s], recv_sem=lf_rsem.at[h, half, s],
            device_id={"seq": down}, device_id_type=MESH,
        )

    for h in range(2):
        for d in range(1, XN):
            for which in range(2):
                kv_copy(d, h, which).start()
        for which in range(2):
            kv_own(h, which).start()
    def start_ring(h):
        for d in range(1, XN):
            for which in range(2):
                kv_copy(d, h, which).wait_recv()
        for which in range(2):
            kv_own(h, which).wait()
        for half in range(2):
            right(h, half, 0).start()
            left(h, half, 0).start()

    def wait_queries(h):
        for d in range(1, XN):
            q_copy(d, h).wait_recv()
        q_own(h).wait()

    lengths = len_ref[pl.ds(dp, 1), :].astype(jnp.float32)
    docs = lengths.shape[1]
    before = (
        lax.broadcasted_iota(jnp.int32, (docs, docs), 1)
        <= lax.broadcasted_iota(jnp.int32, (docs, docs), 0)
    ).astype(jnp.float32)

    def first_position(r):
        return (r * zn + z) * tok

    def token_row(rows):
        lane = lax.broadcasted_iota(jnp.int32, (rows, 2 * tok), 1)
        return jnp.where(lane < tok, lane, lane - tok)

    def find_starts():
        ends = jnp.sum(before * lengths, axis=1, keepdims=True)
        ends = jnp.broadcast_to(ends, (docs, 2 * tok))
        for r in range(XN):
            positions = (first_position(r) + token_row(docs)).astype(jnp.float32)
            first = jnp.max(jnp.where(ends <= positions, ends, 0.0), axis=0, keepdims=True)
            starts[r] = jnp.broadcast_to(first.astype(jnp.int32), (8, 2 * tok))

    def bias_of(r, blocks):
        q_pos = first_position(r) + token_row(tok)
        first = jnp.broadcast_to(starts[r][0:1, :], (tok, 2 * tok))
        key = lax.broadcasted_iota(jnp.int32, (tok, 2 * tok), 0)
        parts = []
        for rk, zk in blocks:
            k_pos = (rk * zn + zk) * tok + key
            ok = (k_pos >= first) & (k_pos <= q_pos)
            parts.append(jnp.where(ok, 0.0, NEG).astype(jnp.float32))
        return jnp.concatenate(parts, axis=0)

    heads_tile = 4
    cols = heads_tile * tok

    def update(h, half, rows, zs, fresh):
        order = [(k, zb) for k in range(2) for zb in zs]
        keys = jnp.concatenate([kvbuf[h, half, zb, 0, k] for k, zb in order], axis=0)
        vals = jnp.concatenate([kvbuf[h, half, zb, 1, k] for k, zb in order], axis=0)
        vals = jnp.concatenate([vals.T, jnp.ones((SUMS, vals.shape[0]), jnp.bfloat16)], axis=0)
        tiles = []
        for r, only_first in rows:
            blocks = order[:len(zs)] if only_first else order
            bias = bias_of(r, [(2 * half + k, zb) for k, zb in blocks])
            bias = jnp.concatenate([bias] * (heads_tile // 2), axis=1)
            for j in range(GROUP // heads_tile):
                tiles.append((r, bias, slice(j * cols, (j + 1) * cols), j * heads_tile * HD))

        def score(tile):
            r, bias, _, lane = tile
            q = qbuf[h, r, :, lane:lane + heads_tile * HD]
            q = jnp.concatenate([q[:, i * HD:(i + 1) * HD] for i in range(heads_tile)], axis=0)
            return lax.dot_general(
                keys[:bias.shape[0]], q, (((1,), (1,)), ((), ())),
                preferred_element_type=jnp.float32,
            )

        old = [None if fresh else mx[h, r, 0:1, at] for r, _, at, _ in tiles]
        tops, prods = [], []
        ahead = [score(tiles[0])]
        for i, (r, bias, at, _) in enumerate(tiles):
            if i + 1 < len(tiles):
                ahead.append(score(tiles[i + 1]))
            s = ahead[i] * scale2 + bias
            top = jnp.max(s, axis=0, keepdims=True)
            if not fresh:
                top = jnp.maximum(old[i], top)
            w = jnp.exp2(s - top).astype(jnp.bfloat16)
            prods.append(
                jnp.dot(vals[:, :bias.shape[0]], w, preferred_element_type=jnp.float32)
            )
            tops.append(top)
        for i, (r, _, at, _) in enumerate(tiles):
            if fresh:
                acc[h, r, :, at] = prods[i]
            else:
                acc[h, r, :, at] = acc[h, r, :, at] * jnp.exp2(old[i] - tops[i]) + prods[i]
            mx[h, r, 0:1, at] = tops[i]

    def work(h, half, zs, fresh=False):
        single = len(zs) == 1
        second, first = (2 * half + 1, False), (2 * half, not single)
        crossing = (2, False)
        if half == 1:
            update(h, half, [second, first], zs, fresh)
        elif fresh:
            update(h, half, [second, first], zs, fresh)

            @pl.when(z == 0)
            def _():
                update(h, half, [crossing], zs, False)
        else:
            @pl.when(z == 0)
            def _():
                update(h, half, [second, crossing], zs, fresh)

            @pl.when(z != 0)
            def _():
                update(h, half, [second, first], zs, fresh)

    def finish(h, r):
        o = acc[h, r, :HD, :] / acc[h, r, HD:HD + 1, :]
        for i in range(GROUP):
            obuf[h, r, :, i * HD:(i + 1) * HD] = o[:, i * tok:(i + 1) * tok].T.astype(jnp.bfloat16)
        for d in range(XN):
            @pl.when(peer(d) == r)
            def _():
                if d:
                    o_copy(d, h).start()
                else:
                    o_own(h).start()

    right_steps = (half_ring, half_ring - 1)
    left_steps = (half_ring - 1, half_ring)

    def forward(h, half, s):
        for copy, steps in ((right, right_steps), (left, left_steps)):
            copy(h, half, s - 1).wait_recv()
            if steps[half] == half_ring:
                copy(h, half, s).start()
            else:
                @pl.when(s < half_ring - 1)
                def _():
                    copy(h, half, s).start()

    def over_heads(body):
        lax.fori_loop(0, 2, lambda h, carry: (body(h), carry)[1], 0)

    def work_pair(h, half, s):
        work(h, half, [(z + zn - s) % zn, (z + s) % zn])

    start_ring(0)
    start_ring(1)
    for d in range(1, XN):
        q_copy(d, 0).start()
    for h in range(2):
        q_own(h).start()
    find_starts()
    ahead = min(2, half_ring - 1)
    for s in range(1, ahead + 1):
        for h in range(2):
            for half in range(2):
                forward(h, half, s)
        if s == 1:
            for d in range(1, XN):
                q_copy(d, 1).start()
    for h in range(2):
        wait_queries(h)
        for half in (1, 0):
            work(h, half, [z], fresh=True)

    def pair_step(h, half, s):
        @pl.when((s >= ahead) & (s < half_ring - 1))
        def _():
            forward(h, half, s + 1)

        work_pair(h, half, s)

    def step(s, carry):
        def heads(h, carry):
            for half in range(2):
                pair_step(h, half, s)
            return carry

        return lax.fori_loop(0, 2, heads, carry)

    lax.fori_loop(1, half_ring, step, 0)
    far = (z + half_ring) % zn

    def drain(h, begin, end):
        for copy, steps in ((right, right_steps), (left, left_steps)):
            for half in range(2):
                def wait_one(s, carry):
                    copy(h, half, s).wait_send()
                    return carry

                lax.fori_loop(begin, end or steps[half], wait_one, 0)

    for h in range(2):
        drain(h, 0, half_ring - 1)
        for d in range(1, XN):
            q_copy(d, h).wait_send()
            for which in range(2):
                kv_copy(d, h, which).wait_send()
    for h in range(2):
        for half in range(2):
            (right if half == 0 else left)(h, half, half_ring - 1).wait_recv()
            work(h, half, [far])
            for r in (2 * half + 1, 2 * half):
                finish(h, r)
    for h in range(2):
        drain(h, half_ring - 1, None)
        for d in range(1, XN):
            o_copy(d, h).wait()
        o_own(h).wait()


def per_device(queries, keys, values, doc_lengths):
    tok = queries.shape[1]
    zn = lax.axis_size("seq") // XN
    dma, vmem = pltpu.SemaphoreType.DMA, pltpu.VMEM
    kvw = GROUP * HD
    return pl.pallas_call(
        functools.partial(kernel, zn, tok),
        out_shape=jax.ShapeDtypeStruct(queries.shape, jnp.bfloat16),
        in_specs=[pl.BlockSpec(memory_space=pl.ANY)] * 3 + [pl.BlockSpec(memory_space=pltpu.VMEM)],
        out_specs=pl.BlockSpec(memory_space=pl.ANY),
        scratch_shapes=[
            vmem((2, XN, tok, kvw), jnp.bfloat16),
            vmem((2, 2, zn, 2, 2, tok, HD), jnp.bfloat16),
            vmem((2, XN, tok, kvw), jnp.bfloat16),
            vmem((2, XN, HD + SUMS, GROUP * tok), jnp.float32),
            vmem((2, XN, 8, GROUP * tok), jnp.float32),
            vmem((XN, 8, 2 * tok), jnp.int32),
            dma((XN - 1, 2, 2)), dma((XN - 1, 2, 2)), dma((2, 2)),
            dma((XN - 1, 2)), dma((XN - 1, 2)), dma((2,)),
            dma((2, 2, zn // 2)), dma((2, 2, zn // 2)),
            dma((2, 2, zn // 2)), dma((2, 2, zn // 2)),
            dma((XN - 1, 2)), dma((XN - 1, 2)), dma((2,)),
        ],
        compiler_params=pltpu.CompilerParams(collective_id=0, has_side_effects=True),
        name="ring_attention",
    )(queries, keys, values, doc_lengths)


def solution(mesh):
    placed = (P("dp", "seq", None), P("dp", "seq", None), P("dp", "seq", None), P())
    return jax.shard_map(
        per_device, mesh=mesh, in_specs=placed, out_specs=P("dp", "seq", None), check_vma=False
    )
```
